32 devices in a mesh: slab: 4 (over y, x), row: 4 (over z), col: 2 (over core).
Axes of the slice: x: 2, y: 2, z: 4, core: 2. Of those that a mesh axis runs over, the one named last changes fastest.
Arguments:
- diagonals: bfloat16 [4, 1024, 1024], P('slab', 'row', 'col'), as said below
- lower_neighbour_coupling: bfloat16 [4, 1024, 1024], P('slab', 'row', 'col'), as said below
- upper_neighbour_coupling: bfloat16 [4, 1024, 1024], P('slab', 'row', 'col'), as said below
- right_hand_columns: bfloat16 [4, 1024, 512], P('slab', 'row', 'col'), may hold values from -6 to 6
Outputs:
- diag_out: bfloat16 [4, 1024, 1024], P('slab', 'row', 'col')
- lower_out: bfloat16 [4, 1024, 1024], P('slab', 'row', 'col')
- upper_out: bfloat16 [4, 1024, 1024], P('slab', 'row', 'col')
- sides_out: bfloat16 [4, 1024, 512], P('slab', 'row', 'col')
The draws below stay inside these ranges and needn't reach their ends.
Inputs may be any that keep to these rules, and one draw needn't show every extreme that they name: Each slab's diagonal block has its diagonal in 1 to 2 and small independent entries off it, so that the pivots of all levels are dominated by their diagonals. `lower_neighbour_coupling`: independent entries of magnitude near 0.2 / sqrt(1024). `upper_neighbour_coupling`: independent entries of magnitude near 0.2 / sqrt(1024).
All inputs are finite; a program needn't handle non-finite values.
Results may differ from the reference program's by a relative error of at most 0.0075.
Values may be sent and summed in bfloat16 or wider, within the bound.
No kernel may reach another device: no remote copies, remote signals or barrier semaphores. Data moves between devices by JAX's collectives and lax.ppermute only.
A program may use at most 64 MiB of HBM per device.

```python
import math
import jax
import jax.numpy as jnp
from jax import lax

BLOCK = 1024
COLUMNS = 512
SWEEPS = 2
SLAB_TOTAL = 4
LEVELS = 1


def coupling_draw(key):
    noise = jnp.clip(jax.random.normal(key, (SLAB_TOTAL, BLOCK, BLOCK), jnp.float32), -4.0, 4.0)
    return (noise * (0.2 / math.sqrt(BLOCK))).astype(jnp.bfloat16)


def draw_diagonals(key, part):
    noise_key, center_key = jax.random.split(jax.random.fold_in(key, 13))
    noise = jnp.clip(jax.random.normal(noise_key, (SLAB_TOTAL, BLOCK, BLOCK), jnp.float32), -4.0, 4.0)
    offdiag = noise * (0.3 / math.sqrt(BLOCK))
    center = jax.random.uniform(center_key, (SLAB_TOTAL, BLOCK), jnp.float32, 1.0, 2.0)
    eye_mask = jnp.eye(BLOCK, dtype=jnp.float32)
    return (offdiag * (1.0 - eye_mask) + eye_mask * center[:, :, None]).astype(jnp.bfloat16)


def draw_lower_neighbour_coupling(key, part):
    return coupling_draw(jax.random.fold_in(key, 11))


def draw_upper_neighbour_coupling(key, part):
    return coupling_draw(jax.random.fold_in(key, 12))


def block_levels(stream_key, shape, cuts, least, top_value):
    level = 1.0
    for axis_at, parts in cuts:
        draws = jax.random.uniform(jax.random.fold_in(jax.random.fold_in(stream_key, 6), axis_at), (parts,), jnp.float32, least / len(cuts), top_value / len(cuts))
        level = level * jnp.repeat(jnp.exp(draws), shape[axis_at] // parts).reshape((-1,) + (1,) * (len(shape) - 1 - axis_at))
    return level


def normal_values(stream_key, shape, scale, reach, pieces=(), held_as=jnp.bfloat16):
    values = scale * jax.random.normal(stream_key, shape, jnp.float32)
    if pieces:
        values = values * block_levels(stream_key, shape, pieces, -0.22, 0.18)
    return jnp.clip(values, -reach, reach).astype(held_as)


def setup_inputs(seed: int = 0) -> dict:
    streams_of = jax.random.split(jax.random.key(seed), 5)
    diagonals = draw_diagonals(jax.random.fold_in(streams_of[4], 71), 0)
    lower_neighbour_coupling = draw_lower_neighbour_coupling(jax.random.fold_in(streams_of[4], 71), 0)
    upper_neighbour_coupling = draw_upper_neighbour_coupling(jax.random.fold_in(streams_of[4], 71), 0)
    right_hand_columns = normal_values(streams_of[3], (SLAB_TOTAL, BLOCK, COLUMNS), 1.0, 6.0, ((0, 4), (1, 4), (2, 2)))
    return {"diagonals": diagonals, "lower_neighbour_coupling": lower_neighbour_coupling, "upper_neighbour_coupling": upper_neighbour_coupling, "right_hand_columns": right_hand_columns}


def jacobi_multiplier(stacked_blocks, pivot_block):
    pivot_full = pivot_block.astype(jnp.float32)
    divisor = jnp.diagonal(pivot_full)
    target = stacked_blocks.astype(jnp.float32)
    iterate = (target / divisor).astype(jnp.bfloat16)
    for sweep_index in range(SWEEPS):
        product = jnp.einsum("akm,mn->akn", iterate.astype(jnp.float32), pivot_full, precision=lax.Precision.HIGHEST)
        iterate = (iterate.astype(jnp.float32) + (target - product) / divisor).astype(jnp.bfloat16)
    return iterate


def reference(diagonals, lower_neighbour_coupling, upper_neighbour_coupling, right_hand_columns):
    zeros_block = jnp.zeros((BLOCK, BLOCK), jnp.bfloat16)
    zeros_wide = jnp.zeros((BLOCK, 2 * BLOCK + COLUMNS), jnp.bfloat16)
    lower_neighbour_coupling = lower_neighbour_coupling.at[0].set(zeros_block)
    upper_neighbour_coupling = upper_neighbour_coupling.at[SLAB_TOTAL - 1].set(zeros_block)
    for level_index in range(LEVELS):
        level_stride = 2 ** level_index
        toward_right = {}
        toward_left = {}
        for eliminate_level in range(SLAB_TOTAL):
            if eliminate_level - level_stride >= 0:
                left_upper_block = upper_neighbour_coupling[eliminate_level - level_stride]
            else:
                left_upper_block = zeros_block
            if eliminate_level + level_stride < SLAB_TOTAL:
                right_lower_block = lower_neighbour_coupling[eliminate_level + level_stride]
            else:
                right_lower_block = zeros_block
            stacked_blocks = jnp.stack([right_lower_block, left_upper_block])
            scaling_factor = jacobi_multiplier(stacked_blocks, diagonals[eliminate_level])
            hand_sides = jnp.concatenate([upper_neighbour_coupling[eliminate_level], lower_neighbour_coupling[eliminate_level], right_hand_columns[eliminate_level]], axis=1).astype(jnp.float32)
            block_products = jnp.einsum("akm,mn->akn", scaling_factor.astype(jnp.float32), hand_sides, precision=lax.Precision.HIGHEST).astype(jnp.bfloat16)
            if eliminate_level + level_stride < SLAB_TOTAL:
                toward_right[eliminate_level + level_stride] = block_products[0]
            if eliminate_level - level_stride >= 0:
                toward_left[eliminate_level - level_stride] = block_products[1]
        new_diag = []
        new_lower = []
        new_upper = []
        new_sides = []
        for keep in range(SLAB_TOTAL):
            from_left = toward_right[keep] if keep in toward_right else zeros_wide
            from_right = toward_left[keep] if keep in toward_left else zeros_wide
            reduced_pivot = diagonals[keep].astype(jnp.float32) - from_left[:, :BLOCK].astype(jnp.float32) - from_right[:, BLOCK:2 * BLOCK].astype(jnp.float32)
            reduced_sides = right_hand_columns[keep].astype(jnp.float32) - from_left[:, 2 * BLOCK:].astype(jnp.float32) - from_right[:, 2 * BLOCK:].astype(jnp.float32)
            new_diag.append(reduced_pivot.astype(jnp.bfloat16))
            new_sides.append(reduced_sides.astype(jnp.bfloat16))
            new_lower.append(-from_left[:, BLOCK:2 * BLOCK])
            new_upper.append(-from_right[:, :BLOCK])
        diagonals = jnp.stack(new_diag)
        right_hand_columns = jnp.stack(new_sides)
        lower_neighbour_coupling = jnp.stack(new_lower)
        upper_neighbour_coupling = jnp.stack(new_upper)
    return diagonals, lower_neighbour_coupling, upper_neighbour_coupling, right_hand_columns
```

```python
import functools

import jax
import jax.numpy as jnp
from jax import lax
from jax.experimental import pallas as pl
from jax.experimental.pallas import tpu as pltpu
from jax.sharding import PartitionSpec as P

SWEEPS = 2


def passed_along(block, axis, distance):
    devices = range(lax.axis_size(axis))
    route = [(i - distance, i) for i in devices if i - distance in devices]
    return lax.ppermute(block, axis, route)


def general_reduction(pivot, lower, upper, sides):
    row_count, col_count = pivot.shape
    slab_count = lax.axis_size("slab")
    slab_position = lax.axis_index("slab")
    row_index = lax.axis_index("row")
    col_index = lax.axis_index("col")
    lower = jnp.where(slab_position == 0, jnp.zeros_like(lower), lower)
    upper = jnp.where(slab_position == slab_count - 1, jnp.zeros_like(upper), upper)
    from_after = passed_along(lower, "slab", -1)
    from_before = passed_along(upper, "slab", 1)
    target = jnp.stack([from_after, from_before]).astype(jnp.float32)
    global_rows = row_index * row_count + lax.broadcasted_iota(jnp.int32, (row_count, col_count), 0)
    global_cols = col_index * col_count + lax.broadcasted_iota(jnp.int32, (row_count, col_count), 1)
    on_diagonal = jnp.where(global_rows == global_cols, pivot.astype(jnp.float32), 0.0)
    divisor = lax.psum(jnp.sum(on_diagonal, axis=0), "row")
    iterate = (target / divisor).astype(jnp.bfloat16)
    pivot_rows = lax.all_gather(pivot, "row", axis=0, tiled=True)
    for sweep_index in range(SWEEPS):
        product = jnp.einsum(
            "akm,mn->akn",
            lax.all_gather(iterate, "col", axis=2, tiled=True),
            pivot_rows,
            preferred_element_type=jnp.float32,
        )
        iterate = (iterate.astype(jnp.float32) + (target - product) / divisor).astype(jnp.bfloat16)
    hand_sides = jnp.concatenate([upper, lower, sides], axis=1)
    products = jnp.einsum(
        "akm,mn->akn",
        lax.all_gather(iterate, "col", axis=2, tiled=True),
        lax.all_gather(hand_sides, "row", axis=0, tiled=True),
        preferred_element_type=jnp.float32,
    ).astype(jnp.bfloat16)
    before = passed_along(products[0], "slab", 1).astype(jnp.float32)
    after = passed_along(products[1], "slab", -1).astype(jnp.float32)
    reduced_pivot = pivot.astype(jnp.float32) - before[:, :col_count] - after[:, col_count : 2 * col_count]
    reduced_sides = sides.astype(jnp.float32) - before[:, 2 * col_count :] - after[:, 2 * col_count :]
    return (
        reduced_pivot.astype(jnp.bfloat16),
        (-before[:, col_count : 2 * col_count]).astype(jnp.bfloat16),
        (-after[:, :col_count]).astype(jnp.bfloat16),
        reduced_sides.astype(jnp.bfloat16),
    )


def block_offset(block, height, half, core):
    start = block * height
    which = start // half
    return pl.multiple_of(lax.rem(which + core, 2) * half + (start - which * half), 128)


def ring_block(step, count):
    return lax.rem(lax.axis_index("row") - step + count, count)


def jacobi_kernel(count, own_ref, other_ref, v_own_ref, v_other_ref, u_ref, inverse_ref, first_ref, second_ref):
    height = own_ref.shape[0] // count
    half = own_ref.shape[1]
    core = lax.axis_index("col")
    eye = lax.broadcasted_iota(jnp.int32, (height, height), 0) == lax.broadcasted_iota(
        jnp.int32, (height, height), 1
    )
    offsets = [block_offset(ring_block(k, count), height, half, core) for k in range(count)]
    for k in range(count):
        inner = pl.multiple_of(lax.rem(offsets[k], half), 128)
        rows = pl.ds(k * height, height)
        here = own_ref[rows, pl.ds(inner, height)].astype(jnp.float32)
        there = other_ref[rows, pl.ds(inner, height)].astype(jnp.float32)
        block = jnp.where(offsets[k] < half, here, there)
        diagonal = jnp.sum(jnp.where(eye, block, 0.0), axis=0, keepdims=True)
        inverse_ref[:, pl.ds(offsets[k], height)] = 1.0 / diagonal
    halves = ((own_ref, v_own_ref, pl.ds(0, half)), (other_ref, v_other_ref, pl.ds(half, half)))
    for _, v_ref, cols in halves:
        first_ref[:, cols] = (v_ref[...].astype(jnp.float32) * inverse_ref[:, cols]).astype(jnp.bfloat16)
    source, spare = first_ref, second_ref
    for sweep_index in range(SWEEPS):
        result = u_ref if sweep_index == SWEEPS - 1 else spare
        for a_ref, v_ref, cols in halves:
            product = jnp.zeros(v_ref.shape, jnp.float32)
            for k in range(count):
                product += jnp.dot(
                    source[:, pl.ds(offsets[k], height)],
                    a_ref[pl.ds(k * height, height), :],
                    preferred_element_type=jnp.float32,
                )
            step = (v_ref[...].astype(jnp.float32) - product) * inverse_ref[:, cols]
            result[:, cols] = (source[:, cols].astype(jnp.float32) + step).astype(jnp.bfloat16)
        source, spare = result, source


def jacobi(own, other, v_own, v_other, count):
    height, half = v_own.shape
    vmem = pl.BlockSpec(memory_space=pltpu.VMEM)
    return pl.pallas_call(
        functools.partial(jacobi_kernel, count),
        out_shape=jax.ShapeDtypeStruct((height, 2 * half), jnp.bfloat16),
        in_specs=[vmem] * 4,
        out_specs=vmem,
        scratch_shapes=[
            pltpu.VMEM((1, 2 * half), jnp.float32),
            pltpu.VMEM((height, 2 * half), jnp.bfloat16),
            pltpu.VMEM((height, 2 * half), jnp.bfloat16),
        ],
        name="jacobi",
    )(own, other, v_own, v_other)


def product_kernel(count, half, zero_slab, u_own_ref, u_given_ref, *refs):
    shards, (q_own_ref, q_given_ref) = refs[:count], refs[count:]
    height = shards[0].shape[0]
    core = lax.axis_index("col")
    for u_ref, q_ref, flip in ((u_own_ref, q_own_ref, core), (u_given_ref, q_given_ref, 1 - core)):
        total = jnp.zeros(q_ref.shape, jnp.float32)
        for k in range(count):
            offset = block_offset(ring_block(k, count), height, half, flip)
            total += jnp.dot(
                u_ref[:, pl.ds(offset, height)], shards[k][...], preferred_element_type=jnp.float32
            )
        if zero_slab is not None:
            total = jnp.where(lax.axis_index("slab") == zero_slab, 0.0, total)
        q_ref[...] = total.astype(jnp.bfloat16)


def schur_products(u_own, u_given, shards, zero_slab):
    vmem = pl.BlockSpec(memory_space=pltpu.VMEM)
    shape = jax.ShapeDtypeStruct((u_own.shape[0], shards[0].shape[1]), jnp.bfloat16)
    return pl.pallas_call(
        functools.partial(product_kernel, len(shards), u_own.shape[1] // 2, zero_slab),
        out_shape=(shape, shape),
        in_specs=[vmem] * (2 + len(shards)),
        out_specs=(vmem, vmem),
        name="schur",
    )(u_own, u_given, *shards)


def tied(value, *others):
    return lax.optimization_barrier((value, *others))[0]


def ring_reduction(pivot, lower, upper, sides):
    slab_count = lax.axis_size("slab")
    row_count = lax.axis_size("row")
    slab = lax.axis_index("slab")
    core = lax.axis_index("col")

    ring = [(i, (i + 1) % row_count) for i in range(row_count)]
    step_on = lambda block: lax.ppermute(block, "row", ring)
    swap = lambda block: lax.ppermute(block, "col", [(0, 1), (1, 0)])

    def near(e):
        return e ^ 1

    def far(e):
        return (e + 1) % slab_count if e % 2 else (e - 1) % slab_count

    index = lambda e, c: 2 * e + c
    partner = lambda e, c: far(e) if c else near(e)
    straight = [(index(e, c), index(partner(e, c), c)) for e in range(slab_count) for c in range(2)]
    opposite = [(index(e, c), index(partner(e, 1 - c), c)) for e in range(slab_count) for c in range(2)]
    crossed = [(index(e, c), index(partner(e, 1 - c), 1 - c)) for e in range(slab_count) for c in range(2)]
    over = lambda block, route: lax.ppermute(block, ("slab", "col"), route)

    masked_lower = jnp.where(slab == 0, jnp.zeros_like(lower), lower)
    masked_upper = jnp.where(slab == slab_count - 1, jnp.zeros_like(upper), upper)
    odd = lax.rem(slab + core, 2) == 1
    to_straight = jnp.where(odd, masked_lower, masked_upper)
    to_crossed = jnp.where(odd, masked_upper, masked_lower)

    a1 = step_on(pivot)
    b1 = step_on(upper)
    v_own = over(to_straight, straight)
    v_other = over(to_crossed, crossed)
    a2 = step_on(a1)
    b2 = step_on(b1)
    a3 = step_on(a2)
    b3 = step_on(b2)
    own = jnp.concatenate([pivot, a1, a2, a3], axis=0)
    other = swap(own)
    c1 = step_on(tied(lower, b2))
    u_own = jacobi(own, other, v_own, v_other, row_count)
    u_given = swap(u_own)
    f1 = step_on(tied(sides, b3))
    c2 = step_on(c1)
    f2 = step_on(f1)
    c3 = step_on(c2)
    f3 = step_on(f2)

    def exchanged(shards, zero_slab):
        q_own, q_given = schur_products(u_own, u_given, shards, zero_slab)
        r_own = over(q_own, straight).astype(jnp.float32)
        r_given = over(q_given, opposite).astype(jnp.float32)
        return jnp.where(odd, r_own, r_given), jnp.where(odd, r_given, r_own)

    before_upper, after_upper = exchanged((upper, b1, b2, b3), slab_count - 1)
    before_lower, after_lower = exchanged((lower, c1, c2, c3), 0)
    before_sides, after_sides = exchanged((sides, f1, f2, f3), None)
    return (
        (pivot.astype(jnp.float32) - before_upper - after_lower).astype(jnp.bfloat16),
        (-before_lower).astype(jnp.bfloat16),
        (-after_upper).astype(jnp.bfloat16),
        (sides.astype(jnp.float32) - before_sides - after_sides).astype(jnp.bfloat16),
    )


def per_device(diagonals, lower_neighbour_coupling, upper_neighbour_coupling, right_hand_columns):
    blocks = (
        diagonals[0],
        lower_neighbour_coupling[0],
        upper_neighbour_coupling[0],
        right_hand_columns[0],
    )
    height, half = blocks[0].shape
    ring_fits = (
        lax.axis_size("col") == 2
        and lax.axis_size("row") == 4
        and lax.axis_size("slab") % 2 == 0
        and height % 128 == 0
        and half % height == 0
    )
    reduced = ring_reduction(*blocks) if ring_fits else general_reduction(*blocks)
    return tuple(block[None] for block in reduced)


def solution(mesh):
    placed = (P("slab", "row", "col"),) * 4
    return jax.shard_map(per_device, mesh=mesh, in_specs=placed, out_specs=placed, check_vma=False)
```
